32 devices in a mesh: vel: 8 (over z, x), cell: 4 (over y, core).
Axes of the slice: x: 2, y: 2, z: 4, core: 2. Of those that a mesh axis runs over, the one named last changes fastest.
Arguments:
- distribution: float32 [13824, 512], P('vel', 'cell'), may hold values from 0.2 to 2
- pair_first: int32 [8, 8, 256], P('vel'), may hold values from 0 to 1727
- pair_second: int32 [8, 8, 256], P('vel'), may hold values from 0 to 1727
- pair_weight: float32 [8, 8, 256], P('vel'), may hold values from 0.05 to 0.5
- proj_pair: int32 [8, 8, 8, 64], P('vel'), may hold values from 0 to 255
- proj_target: int32 [8, 8, 8, 64], P(None, None, 'vel'), may hold values from 0 to 1727
- proj_coef: float32 [8, 8, 8, 64], P(None, None, 'vel'), may hold values from 0.1 to 1
- slot_counts: int32 [8, 8, 8], P(None, None, 'vel'), may hold values from 16 to 64, as said below
Outputs:
- transported: float32 [13824, 512], P('vel', 'cell')
- collision: float32 [13824, 512], P('vel', 'cell')
The draws below stay inside these ranges and needn't reach their ends.
Inputs may be any that keep to these rules, and one draw needn't show every extreme that they name: slot_counts[s, p, o] live slots, counted from the first, in the list that source group s fills for partner group p and owner group o; for every offset (s - p) mod 8 one owner group gets exactly 64 live slots from every source group.
All inputs are finite; a program needn't handle non-finite values.
Results may differ from the reference program's by a relative error of at most 0.000054.
Values sent between devices are 32-bit elements; how exact they have to be, the bound alone decides.
No kernel may reach another device: no remote copies, remote signals or barrier semaphores. Data moves between devices by JAX's collectives and lax.ppermute only.
A program may use at most 64 MiB of HBM per device.

```python
import math
import jax
import jax.numpy as jnp
from jax import lax

VSIDE = 24
PB = 256
V = 13824
GROUPS = 8
VB = 1728
SLOTS = 64
CELLS = 512


def draw_slot_counts(key, part):
    heavy_owner = jax.random.randint(jax.random.fold_in(key, 11), (GROUPS,), 0, GROUPS)
    base_count = jax.random.randint(jax.random.fold_in(key, 12), (GROUPS, GROUPS, GROUPS), SLOTS // 4, 3 * SLOTS // 4 + 1)
    source = jnp.arange(GROUPS)[:, None, None]
    partner = jnp.arange(GROUPS)[None, :, None]
    owner_index = jnp.arange(GROUPS)[None, None, :]
    offset = (source - partner) % GROUPS
    return jnp.where(owner_index == heavy_owner[offset], SLOTS, base_count).astype(jnp.int32)


def plant(result, own_key, low, top_value):
    spot = [jax.random.randint(jax.random.fold_in(own_key, axis), (), 0, length) for axis, length in enumerate(result.shape)]
    widest = result.shape.index(max(result.shape))
    next_to = spot[:widest] + [(spot[widest] + 1) % result.shape[widest]] + spot[widest + 1:]
    return result.at[tuple(spot)].set(low).at[tuple(next_to)].set(top_value)


def block_scale(own_key, shape, cuts, low, top_value):
    gain = 1.0
    for axis_at, blocks in cuts:
        steps = jax.random.uniform(jax.random.fold_in(jax.random.fold_in(own_key, 6), axis_at), (blocks,), jnp.float32, low / len(cuts), top_value / len(cuts))
        gain = gain * jnp.repeat(jnp.exp(steps), shape[axis_at] // blocks).reshape((-1,) + (1,) * (len(shape) - 1 - axis_at))
    return gain


def setup_inputs(seed: int = 0) -> dict:
    keys = jax.random.split(jax.random.key(seed), 9)
    distribution = jnp.clip(jnp.exp(math.log(2.0) - 2.3025851 * jax.random.uniform(keys[0], (V, CELLS), jnp.float32) ** block_scale(keys[0], (V, CELLS), ((0, 8), (1, 4)), -0.2, 0.2)), 0.2, 2.0)
    pair_first = plant(jax.random.randint(keys[1], (GROUPS, GROUPS, PB), 0, VB), jax.random.fold_in(keys[1], 1), 0, VB - 1).astype(jnp.int32)
    pair_second = plant(jax.random.randint(keys[2], (GROUPS, GROUPS, PB), 0, VB), jax.random.fold_in(keys[2], 1), 0, VB - 1).astype(jnp.int32)
    pair_weight = jnp.clip(jnp.exp(math.log(0.5) - 2.3025851 * jax.random.uniform(keys[3], (GROUPS, GROUPS, PB), jnp.float32) ** block_scale(keys[3], (GROUPS, GROUPS, PB), ((0, 8),), -0.2, 0.2)), 0.05, 0.5)
    proj_pair = plant(jax.random.randint(keys[4], (GROUPS, GROUPS, GROUPS, SLOTS), 0, PB), jax.random.fold_in(keys[4], 1), 0, PB - 1).astype(jnp.int32)
    proj_target = plant(jax.random.randint(keys[5], (GROUPS, GROUPS, GROUPS, SLOTS), 0, VB), jax.random.fold_in(keys[5], 1), 0, VB - 1).astype(jnp.int32)
    proj_coef = jnp.clip(0.1 + 0.9 * jax.random.uniform(keys[6], (GROUPS, GROUPS, GROUPS, SLOTS), jnp.float32) ** block_scale(keys[6], (GROUPS, GROUPS, GROUPS, SLOTS), ((2, 8),), -0.2, 0.2), 0.1, 1.0)
    slot_counts = draw_slot_counts(jax.random.fold_in(keys[8], 71), 0)
    return dict(distribution=distribution, pair_first=pair_first, pair_second=pair_second, pair_weight=pair_weight, proj_pair=proj_pair, proj_target=proj_target, proj_coef=proj_coef, slot_counts=slot_counts)


def reference(distribution, pair_first, pair_second, pair_weight, proj_pair, proj_target, proj_coef, slot_counts):
    block_rows = V // GROUPS
    node_index = jnp.arange(V, dtype=jnp.int32)
    first_axis = node_index // (VSIDE * VSIDE)
    courant = ((2 * first_axis - VSIDE + 1) / (2.0 * VSIDE)).astype(jnp.float32)[:, None]
    left_cell = jnp.roll(distribution, 1, axis=1)
    right_cell = jnp.roll(distribution, -1, axis=1)
    transported = distribution - jnp.maximum(courant, 0.0) * (distribution - left_cell) - jnp.minimum(courant, 0.0) * (right_cell - distribution)
    slot_index = jnp.arange(SLOTS, dtype=jnp.int32)
    owner_start = (jnp.arange(GROUPS, dtype=jnp.int32) * block_rows)[:, None]

    def advance(pair_block, totals):
        loss_sum, gain_sum = totals
        source = (pair_block // GROUPS).astype(jnp.int32)
        partner = (pair_block % GROUPS).astype(jnp.int32)
        first_node = pair_first[source, partner] + source * block_rows
        second_node = pair_second[source, partner] + partner * block_rows
        product = pair_weight[source, partner][:, None] * transported[first_node] * transported[second_node]
        loss_sum = loss_sum.at[first_node].add(product)
        live_slot = slot_index[None, :] < slot_counts[source, partner][:, None]
        factors = jnp.where(live_slot, proj_coef[source, partner], jnp.zeros_like(proj_coef[source, partner]))
        values = product[proj_pair[source, partner]] * factors[:, :, None]
        target = proj_target[source, partner] + owner_start
        gain_sum = gain_sum.at[target.reshape(-1)].add(values.reshape(-1, values.shape[-1]))
        return loss_sum, gain_sum

    zeros = jnp.zeros_like(transported)
    loss_sum, gain_sum = lax.fori_loop(0, GROUPS * GROUPS, advance, (zeros, zeros))
    return transported, gain_sum - loss_sum
```

```python
import functools

import jax
import jax.numpy as jnp
from jax import lax
from jax.experimental import pallas as pl
from jax.experimental.pallas import tpu as pltpu
from jax.sharding import PartitionSpec as P

VSIDE = 24
LANE = 128
FOLD = 256
VMEM_SPEC = pl.BlockSpec(memory_space=pltpu.VMEM)


def whole_call(body, out_shape, scratch=(), name=None):
    multiple = isinstance(out_shape, (tuple, list))
    return pl.pallas_call(
        body,
        out_shape=out_shape,
        out_specs=tuple(VMEM_SPEC for _ in out_shape) if multiple else VMEM_SPEC,
        scratch_shapes=list(scratch),
        name=name,
    )


def padded_block(x, rows):
    if x.shape[0] == rows:
        return x
    return jnp.concatenate([x, jnp.zeros((rows - x.shape[0], x.shape[1]), x.dtype)], axis=0)


def flip_kernel(nodes, x_ref, y_ref, head_ref, tail_ref):
    cells, padded = y_ref.shape
    for start in range(0, padded, LANE):
        if start >= nodes:
            y_ref[:, start : start + LANE] = jnp.zeros((cells, LANE), jnp.float32)
        else:
            stop = min(start + LANE, nodes)
            y_ref[:, start : start + LANE] = padded_block(x_ref[start:stop, :], LANE).T
    head_ref[...] = y_ref[0:1, :]
    tail_ref[...] = y_ref[cells - 1 : cells, :]


def transport_kernel(x_ref, left_ref, right_ref, courant_ref, y_ref):
    x = x_ref[...]
    courant = courant_ref[...]
    left = jnp.concatenate([left_ref[...], x[:-1]], axis=0)
    right = jnp.concatenate([x[1:], right_ref[...]], axis=0)
    y_ref[...] = x - jnp.maximum(courant, 0.0) * (x - left) - jnp.minimum(courant, 0.0) * (right - x)


def unflip_kernel(nodes, x_ref, y_ref):
    for start in range(0, nodes, LANE):
        stop = min(start + LANE, nodes)
        y_ref[start:stop, :] = x_ref[:, start : start + LANE].T[: stop - start]


def scatter_rows(values, target_rows, folds):
    cells, count = values.shape
    high = values.astype(jnp.bfloat16)
    low = (values - high.astype(jnp.float32)).astype(jnp.bfloat16)
    target = jnp.concatenate(target_rows, axis=1)
    fold = jnp.floor(target * (1.0 / FOLD))
    lane = target - fold * FOLD
    fold = jnp.broadcast_to(fold, (cells, count)).astype(jnp.bfloat16)
    lane = jnp.broadcast_to(lane, (FOLD, count)).astype(jnp.bfloat16)
    index = lax.broadcasted_iota(jnp.int32, (FOLD, count), 0).astype(jnp.bfloat16)
    one_hot = jnp.where(lane == index, jnp.ones_like(lane), jnp.zeros_like(lane))
    zero = jnp.zeros_like(high)
    masks = [fold == jnp.bfloat16(f) for f in range(folds)]
    stacked = jnp.concatenate(
        [jnp.where(m, high, zero) for m in masks] + [jnp.where(m, low, zero) for m in masks], axis=0
    )
    sums = lax.dot_general(
        stacked, one_hot, (((1,), (1,)), ((), ())), preferred_element_type=jnp.float32
    )
    return sums[: folds * cells] + sums[folds * cells :]


def pick(block, lane):
    return jnp.take_along_axis(block, lane, axis=1, mode="promise_in_bounds")


def collide_kernel(groups, pairs, slots, t_ref, index_ref, out_ref, product_ref, total_ref):
    _, cells, padded = t_ref.shape
    folds = padded // FOLD
    blocks = padded // LANE
    tiles = pairs // LANE
    pair_rows = groups * tiles
    slot_rows = groups * slots // LANE
    at_second = pair_rows
    at_weight = 2 * pair_rows
    at_pair = 3 * pair_rows
    at_target = at_pair + groups * slot_rows
    at_coef = at_target + groups * slot_rows
    per_row = LANE // slots
    total_ref[...] = jnp.zeros_like(total_ref)

    def split_index(row):
        index = jnp.broadcast_to(row, (8, LANE)).astype(jnp.int32)
        return index & (LANE - 1), index // LANE

    def pick_node(group, first_cell, lane, block):
        result = None
        for b in range(blocks):
            found = pick(t_ref[group, first_cell : first_cell + 8, b * LANE : (b + 1) * LANE], lane)
            result = found if b == 0 else jnp.where(block == b, found, result)
        return result

    def from_source(source, carry):
        def with_partner(partner, carry):
            for j in range(tiles):
                row = partner * tiles + j
                first = split_index(index_ref[source, pl.ds(row, 1), :])
                second = split_index(index_ref[source, pl.ds(at_second + row, 1), :])
                weight = index_ref[source, pl.ds(at_weight + row, 1), :]
                for c in range(0, cells, 8):
                    product_ref[partner, j, c : c + 8, :] = (
                        weight * pick_node(source, c, *first) * pick_node(partner, c, *second)
                    )
            return carry

        lax.fori_loop(0, groups, with_partner, 0)

        def add_loss(half, carry):
            values, rows = [], []
            for partner in (2 * half, 2 * half + 1):
                for j in range(tiles):
                    values.append(-product_ref[partner, j])
                    rows.append(index_ref[source, pl.ds(partner * tiles + j, 1), :])
            total_ref[source] += scatter_rows(jnp.concatenate(values, axis=1), rows, folds)
            return carry

        lax.fori_loop(0, groups // 2, add_loss, 0)
        position = lax.broadcasted_iota(jnp.int32, (8, LANE), 1) // slots

        def add_gain(owner, carry):
            values, rows = [], []
            for r in range(slot_rows):
                lane, tile = split_index(index_ref[source, pl.ds(at_pair + owner * slot_rows + r, 1), :])
                coef = index_ref[owner, pl.ds(at_coef + source * slot_rows + r, 1), :]
                column = []
                for c in range(0, cells, 8):
                    result = None
                    for q in range(per_row):
                        for j in range(tiles):
                            found = pick(product_ref[r * per_row + q, j, c : c + 8, :], lane)
                            mine = (tile == j) & (position == q)
                            result = found if result is None else jnp.where(mine, found, result)
                    column.append(result * coef)
                values.append(jnp.concatenate(column, axis=0))
                rows.append(index_ref[owner, pl.ds(at_target + source * slot_rows + r, 1), :])
            total_ref[owner] += scatter_rows(jnp.concatenate(values, axis=1), rows, folds)
            return carry

        lax.fori_loop(0, groups, add_gain, 0)
        return carry

    lax.fori_loop(0, groups, from_source, 0)
    for owner in range(groups):
        for f in range(folds):
            out_ref[owner, :, f * FOLD : (f + 1) * FOLD] = total_ref[
                owner, f * cells : (f + 1) * cells, :
            ]


def on_device(
    distribution,
    pair_first,
    pair_second,
    pair_weight,
    proj_pair,
    proj_target,
    proj_coef,
    slot_counts,
):
    nodes, cells = distribution.shape
    groups = lax.axis_size("vel")
    position = lax.axis_index("vel")
    pairs = pair_first.shape[2]
    slots = proj_target.shape[3]
    padded = -(-nodes // FOLD) * FOLD
    part = cells // groups
    f32 = jnp.float32

    live = jnp.arange(slots, dtype=jnp.int32) < slot_counts[:, :, :, None]
    coef = jnp.where(live, proj_coef, 0.0)
    table = jnp.concatenate(
        [
            pair_first.reshape(-1, LANE).astype(f32),
            pair_second.reshape(-1, LANE).astype(f32),
            pair_weight.reshape(-1, LANE),
            proj_pair[0].transpose(1, 0, 2).reshape(-1, LANE).astype(f32),
            proj_target.reshape(-1, LANE).astype(f32),
            coef.reshape(-1, LANE),
        ],
        axis=0,
    )
    tables = lax.all_to_all(
        jnp.broadcast_to(table[None], (groups,) + table.shape), "vel", 0, 0, tiled=True
    )

    node = position * nodes + jnp.arange(padded, dtype=jnp.int32)
    courant = ((2 * (node // (VSIDE * VSIDE)) - VSIDE + 1) / (2.0 * VSIDE)).astype(f32)[None, :]
    edge = jax.ShapeDtypeStruct((1, padded), f32)
    flat = jax.ShapeDtypeStruct((cells, padded), f32)
    turned, head, tail = whole_call(
        functools.partial(flip_kernel, nodes), (flat, edge, edge), name="flip"
    )(distribution)
    count = lax.axis_size("cell")
    left = lax.ppermute(tail, "cell", [(i, (i + 1) % count) for i in range(count)])
    right = lax.ppermute(head, "cell", [((i + 1) % count, i) for i in range(count)])
    moved = whole_call(transport_kernel, flat, name="transport")(turned, left, right, courant)
    back = whole_call(
        functools.partial(unflip_kernel, nodes), jax.ShapeDtypeStruct((nodes, cells), f32), name="unflip"
    )
    everywhere = lax.all_to_all(moved.reshape(groups, part, padded), "vel", 0, 0, tiled=True)
    transported = back(moved)
    change = whole_call(
        functools.partial(collide_kernel, groups, pairs, slots),
        jax.ShapeDtypeStruct((groups, part, padded), f32),
        scratch=[
            pltpu.VMEM((groups, pairs // LANE, part, LANE), f32),
            pltpu.VMEM((groups, padded // FOLD * part, FOLD), f32),
        ],
        name="collide",
    )(everywhere, tables)
    owned = lax.all_to_all(change, "vel", 0, 0, tiled=True)
    collision = back(owned.reshape(cells, padded))
    return transported, collision


def solution(mesh):
    in_specs = (
        P("vel", "cell"),
        P("vel", None, None),
        P("vel", None, None),
        P("vel", None, None),
        P("vel", None, None, None),
        P(None, None, "vel", None),
        P(None, None, "vel", None),
        P(None, None, "vel"),
    )
    out_specs = (P("vel", "cell"), P("vel", "cell"))
    return jax.shard_map(
        on_device, mesh=mesh, in_specs=in_specs, out_specs=out_specs, check_vma=False
    )
```
